256 devices in a mesh: grp: 4 (over y), col: 64 (over z, x, core).
Axes of the slice: x: 4, y: 4, z: 8, core: 2. Of those that a mesh axis runs over, the one named last changes fastest.
Arguments:
- orbitals: bfloat16 [2, 6656, 4096], P(None, 'col', 'grp'), may hold values from -6 to 6
- cosine_tiles: bfloat16 [256, 256, 256], P(('grp', 'col')), may hold values from -0.046875 to 0.046875
- sine_tiles: bfloat16 [256, 256, 256], P(('grp', 'col')), may hold values from -0.046875 to 0.046875
- tile_row: int32 [256], P('grp'), may hold values from -1 to 3, as said below
- tile_col: int32 [256], P('grp'), may hold values from -1 to 15, as said below
- row_place: int32 [16], replicated, may hold values from 0 to 15, each once
Outputs:
- propagated: bfloat16 [2, 6656, 4096], P(None, 'col', 'grp')
The draws below stay inside these ranges and needn't reach their ends.
Inputs may be any that keep to these rules, and one draw needn't show every extreme that they name: `tile_row`: slot t belongs to group t // 64; a used slot names one of the group's 4 block rows; empty slots are -1 here and in tile_col at the same places; every group uses two fifths of its 64 slots or more, some group all of them, and a group's used slots lie anywhere among its slots. Two slots may name the same tile position, and their tiles then add. `tile_col`: A used slot names any initial block column of the slab. Initial block row p is stored as storage block row_place[p], in group row_place[p] // 4.
All inputs are finite; a program needn't handle non-finite values.
Results may differ from the reference program's by a relative error of at most 0.005.
Values may be sent and summed in bfloat16 or wider, within the bound.
No kernel may reach another device: no remote copies, remote signals or barrier semaphores. Data moves between devices by JAX's collectives and lax.ppermute only.
A program may use at most 128 MiB of HBM per device.

```python
import jax
import jax.numpy as jnp
from jax import lax

TILE = 256
ORB = 6656
RPG = 4
STEPS = 2
GCAP = 64
NB = 16
NROWS = 4096
N_GRP = 4


def group_ranking(subkey):
    return jax.random.permutation(subkey, GCAP)


def tile_lists(key):
    folded = jax.random.fold_in(key, 31)
    count_key, full_key, rank_key, row_key, col_key = jax.random.split(folded, 5)
    counts = jax.random.randint(count_key, (N_GRP,), (2 * GCAP + 4) // 5, GCAP + 1)
    full_group = jax.random.randint(full_key, (), 0, N_GRP)
    counts = jnp.where(jnp.arange(N_GRP) == full_group, GCAP, counts)
    ranking = jax.vmap(group_ranking)(jax.random.split(rank_key, N_GRP))
    occupied = ranking < counts[:, None]
    row_draw = jax.random.randint(row_key, (N_GRP, GCAP), 0, RPG)
    col_draw = jax.random.randint(col_key, (N_GRP, GCAP), 0, NB)
    rows_out = jnp.where(occupied, row_draw, -1).reshape(N_GRP * GCAP).astype(jnp.int32)
    cols_out = jnp.where(occupied, col_draw, -1).reshape(N_GRP * GCAP).astype(jnp.int32)
    return (rows_out, cols_out)


def draw_tile_row(key, part):
    return tile_lists(key)[0]


def draw_tile_col(key, part):
    return tile_lists(key)[1]


def shard_levels(stream_key, extent, shards, least, high):
    loudness, own = 1.0, jax.random.fold_in(stream_key, 6)
    for dim, parts in shards:
        draws = jnp.exp(jax.random.uniform(jax.random.fold_in(own, dim), (parts,), jnp.float32, least / len(shards), high / len(shards)))
        loudness = loudness * jnp.repeat(draws, extent[dim] // parts).reshape([-1 if axis == dim else 1 for axis in range(len(extent))])
    return loudness


def centred(key, dims, scale, most, shards=(), held_as=jnp.bfloat16):
    factor_of = shard_levels(key, dims, shards, -0.22, 0.18) if shards else 1.0
    array = jax.random.normal(key, dims, jnp.float32) * scale * factor_of
    return jnp.minimum(jnp.maximum(array, -most), most).astype(held_as)


def setup_inputs(seed: int = 0) -> dict:
    keys = jax.random.split(jax.random.key(seed), 7)
    return {
        "orbitals": centred(keys[0], (2, ORB, NROWS), 1.0, 6.0, ((1, 64), (2, 4))),
        "cosine_tiles": centred(keys[1], (N_GRP * GCAP, TILE, TILE), (4 * GCAP * TILE // RPG) ** -0.5, 0.046875, ((0, 256),)),
        "sine_tiles": centred(keys[2], (N_GRP * GCAP, TILE, TILE), (4 * GCAP * TILE // RPG) ** -0.5, 0.046875, ((0, 256),)),
        "tile_row": draw_tile_row(jax.random.fold_in(keys[6], 71), 0),
        "tile_col": draw_tile_col(jax.random.fold_in(keys[6], 71), 0),
        "row_place": jax.random.permutation(keys[5], NB).astype(jnp.int32),
    }


def apply_tiles(panels, tiles, tile_row, source_block):
    def one_group(group_data):
        group_tiles, group_rows, group_source = group_data
        chosen = jnp.take(panels, group_source, axis=1).astype(jnp.float32)
        product = jnp.einsum("osj,sij->osi", chosen, group_tiles.astype(jnp.float32), precision=lax.Precision.HIGHEST)
        onehot = (group_rows[:, None] == jnp.arange(RPG, dtype=jnp.int32)[None, :]).astype(jnp.float32)
        return jnp.einsum("osi,sr->ori", product, onehot, precision=lax.Precision.HIGHEST)

    stacked = lax.map(one_group, (tiles.reshape(N_GRP, GCAP, TILE, TILE), tile_row.reshape(N_GRP, GCAP), source_block.reshape(N_GRP, GCAP)))
    return jnp.transpose(stacked, (1, 0, 2, 3)).reshape(stacked.shape[1], NB, TILE)


def reference(orbitals, cosine_tiles, sine_tiles, tile_row, tile_col, row_place):
    source_block = jnp.where(tile_col >= 0, jnp.take(row_place, jnp.clip(tile_col, 0, NB - 1)), 0).astype(jnp.int32)
    current = orbitals.reshape(2 * ORB, NB, TILE)
    for update in range(STEPS):
        spread = apply_tiles(current, cosine_tiles, tile_row, source_block).astype(jnp.bfloat16)
        cosine_part = apply_tiles(spread, cosine_tiles, tile_row, source_block)
        sine_part = apply_tiles(spread, sine_tiles, tile_row, source_block)
        previous = current.astype(jnp.float32)
        real_new = 2.0 * (cosine_part[:ORB] + sine_part[ORB:]) - previous[:ORB]
        imag_new = 2.0 * (cosine_part[ORB:] - sine_part[:ORB]) - previous[ORB:]
        current = jnp.concatenate([real_new, imag_new], axis=0).astype(jnp.bfloat16)
    return current.reshape(2, ORB, NROWS)
```

```python
import functools

import jax
import jax.numpy as jnp
from jax import lax
from jax.experimental import pallas as pl
from jax.experimental.pallas import tpu as pltpu
from jax.sharding import PartitionSpec as P

STEPS = 2
NZ, NX, NY = 8, 4, 4
MIB = 1024 * 1024


def chip_moves(dz, dx):
    pairs = []
    for c in range(NZ * NX * 2):
        z, x, k = c // (2 * NX), (c // 2) % NX, c % 2
        pairs.append((c, (((z + dz) % NZ) * NX + (x + dx) % NX) * 2 + k))
    return pairs


def move_z(a, s):
    return lax.ppermute(a, "col", chip_moves(s, 0))


def move_x(a, s):
    return lax.ppermute(a, "col", chip_moves(0, s))


def move_y(a, s):
    return lax.ppermute(a, "grp", [(i, (i + s) % NY) for i in range(NY)])


def swap_cores(a):
    return lax.ppermute(a, "col", [(c, c ^ 1) for c in range(NZ * NX * 2)])


def ring(a, move, n):
    out, p, m = [a], a, a
    for _ in range(n // 2 - 1):
        p, m = move(p, 1), move(m, -1)
        out += [p, m]
    h = a.shape[0] // 2
    return out + [move(p[:h], 1), move(m[h:], -1)]


def ring_offsets(n):
    out = [0]
    for d in range(1, n // 2):
        out += [-d, d]
    return out + [n // 2]


def scatter_kernel(counts, meta, *refs):
    pieces, out, acc = refs[: len(counts)], refs[-2], refs[-1]
    rows = out.shape[0]
    step = 64

    def clear(i, _):
        acc[pl.ds(pl.multiple_of(i * step, step), step), :] = jnp.zeros((step, acc.shape[1]), jnp.float32)
        return 0

    lax.fori_loop(0, rows // step, clear, 0)
    at = 0
    for ref, n in zip(pieces, counts):
        def add(t, _, ref=ref, at=at):
            r = meta[0, at + t]

            @pl.when(r >= 0)
            def _():
                row = pl.ds(pl.multiple_of(r * 128, 128), 128)
                for h in range(2):
                    lane = pl.ds(pl.multiple_of(meta[1 + h, at + t] * 128, 128), 128)
                    acc[row, lane] += ref[t, :, h * 128 : (h + 1) * 128].astype(jnp.float32)

            return 0

        lax.fori_loop(0, n, add, 0)
        at += n

    def done(i, _):
        row = pl.ds(pl.multiple_of(i * step, step), step)
        out[row, :] = acc[row, :].astype(jnp.bfloat16)
        return 0

    lax.fori_loop(0, rows // step, done, 0)


def vmem():
    return pl.BlockSpec(memory_space=pltpu.VMEM)


def scatter(meta, pieces):
    counts = tuple(p.shape[0] for p in pieces)
    return pl.pallas_call(
        functools.partial(scatter_kernel, counts),
        out_shape=jax.ShapeDtypeStruct((512, 4096), jnp.bfloat16),
        in_specs=[pl.BlockSpec(memory_space=pltpu.SMEM)] + [vmem()] * len(pieces),
        out_specs=vmem(),
        scratch_shapes=[pltpu.VMEM((512, 4096), jnp.float32)],
        compiler_params=pltpu.CompilerParams(vmem_limit_bytes=24 * MIB),
        cost_estimate=pl.CostEstimate(flops=0, bytes_accessed=12 * MIB, transcendentals=0),
        name="scatter",
    )(meta, *pieces)


def nt(a, b):
    return lax.dot_general(a, b, (((1,), (1,)), ((), ())), preferred_element_type=jnp.float32)


def product(x, b_ref, cols):
    own, p, m, fp, fm = x[0:5], x[5:10], None, None, None
    total = None
    for h, part in enumerate((x[0:5], x[5:10])):
        for g in range(3):
            q = (g * 2 + h) * 512
            d = nt(part[g][...], b_ref[cols, q : q + 512])
            total = d if total is None else total + d
        q = (6 + h) * 512
        b = b_ref[cols, q : q + 512]
        total = total + jnp.concatenate([nt(part[3][...], b), nt(part[4][...], b)], axis=0)
    return total


def spread_kernel(*refs):
    x, c_ref, out = refs[:10], refs[10], refs[11]

    def body(j, _):
        cols = pl.ds(pl.multiple_of(j * 256, 256), 256)
        out[:, cols] = product(x, c_ref, cols).astype(jnp.bfloat16)
        return 0

    lax.fori_loop(0, 2, body, 0)


def step_kernel(*refs):
    x, c_ref, s_ref, cur, out = refs[:10], refs[10], refs[11], refs[12], refs[13]
    half = cur.shape[0] // 2

    def body(j, _):
        cols = pl.ds(pl.multiple_of(j * 256, 256), 256)
        c = product(x, c_ref, cols)
        s = product(x, s_ref, cols)
        prev = cur[:, cols].astype(jnp.float32)
        out[:half, cols] = (2.0 * (c[:half] + s[half:]) - prev[:half]).astype(jnp.bfloat16)
        out[half:, cols] = (2.0 * (c[half:] - s[:half]) - prev[half:]).astype(jnp.bfloat16)
        return 0

    lax.fori_loop(0, 2, body, 0)


def run(kernel, args, flops, name):
    return pl.pallas_call(
        kernel,
        out_shape=jax.ShapeDtypeStruct((416, 512), jnp.bfloat16),
        in_specs=[vmem()] * len(args),
        out_specs=vmem(),
        compiler_params=pltpu.CompilerParams(vmem_limit_bytes=24 * MIB),
        cost_estimate=pl.CostEstimate(flops=flops, bytes_accessed=8 * MIB, transcendentals=0),
        name=name,
    )(*args)


def exchange(cur):
    h = cur.shape[0] // 2
    p, m = move_y(cur, 1), move_y(cur, -1)
    fp, fm = move_y(p[:h], 1), move_y(m[h:], -1)
    got = [cur, p, m, fp, fm]
    return got + [swap_cores(v) for v in got]


def on_device(orbitals, cosine_tiles, sine_tiles, tile_row, tile_col, row_place):
    col = lax.axis_index("col")
    grp = lax.axis_index("grp")
    k = col % 2
    z, x = col // (2 * NX), (col // 2) % NX
    both = jnp.concatenate([cosine_tiles, sine_tiles], axis=0)
    keep = jnp.where(k == 0, both[:, :128], both[:, 128:])
    send = jnp.where(k == 0, both[:, 128:], both[:, :128])
    got = swap_cores(send)
    c2 = jnp.stack([keep[0], got[0]])
    s2 = jnp.stack([keep[1], got[1]])
    c16 = jnp.concatenate(ring(c2, move_z, NZ))
    s8 = jnp.concatenate(ring(s2, move_x, NX))
    s8, c16 = lax.optimization_barrier((s8, c16))
    c_all = ring(c16, move_x, NX)
    s_all = ring(s8, move_z, NZ)

    def meta_of(zs, xs):
        slot = ((z + zs) % NZ * NX + (x + xs) % NX)[:, None] * 2 + (k ^ jnp.arange(2))[None, :]
        hit = slot.reshape(-1)[:, None] == jnp.arange(64, dtype=jnp.int32)[None, :]
        row = jnp.sum(jnp.where(hit, tile_row[None, :], 0), axis=1)
        tcol = jnp.sum(jnp.where(hit, tile_col[None, :], 0), axis=1)
        blk = jnp.sum(
            jnp.where(tcol[:, None] == jnp.arange(16, dtype=jnp.int32)[None, :], row_place[None, :], 0), axis=1
        )
        d = (blk // 4 - grp) % 4
        grel = jnp.where(d == 0, 0, jnp.where(d == 3, 1, d + 1))
        base = grel * 8 + blk % 4
        return jnp.stack([row, base + 4 * k, base + 4 * (1 - k)]).astype(jnp.int32)

    zo, xo = jnp.array(ring_offsets(NZ), jnp.int32), jnp.array(ring_offsets(NX), jnp.int32)
    c_meta = meta_of(jnp.tile(zo, NX), jnp.repeat(xo, NZ))
    s_meta = meta_of(jnp.repeat(zo, NX), jnp.tile(xo, NZ))

    o = orbitals.reshape(2, 104, 4, 2, 128)
    mine = jnp.where(k == 0, o[:, :, :, 0], o[:, :, :, 1]).reshape(2, 104, 512)
    away = jnp.where(k == 0, o[:, :, :, 1], o[:, :, :, 0]).reshape(2, 104, 512)
    part = swap_cores(away)
    first, second = jnp.where(k == 0, mine, part), jnp.where(k == 0, part, mine)
    cur = jnp.stack([first, second], axis=1).reshape(416, 512)

    panels = exchange(cur)
    c_mat = scatter(c_meta, c_all)
    flops = 2 * 416 * 4096 * 512
    spread = run(spread_kernel, panels + [c_mat], flops, "spread")
    s_mat = scatter(s_meta, s_all)
    for update in range(STEPS):
        if update:
            spread = run(spread_kernel, exchange(cur) + [c_mat], flops, "spread")
        cur = run(step_kernel, exchange(spread) + [c_mat, s_mat, cur], 2 * flops, "step")

    c4 = cur.reshape(2, 2, 104, 512)
    mine = jnp.where(k == 0, c4[:, 0], c4[:, 1])
    away = jnp.where(k == 0, c4[:, 1], c4[:, 0])
    part = swap_cores(away)
    lo, hi = jnp.where(k == 0, mine, part), jnp.where(k == 0, part, mine)
    return jnp.stack([lo.reshape(2, 104, 4, 128), hi.reshape(2, 104, 4, 128)], axis=3).reshape(2, 104, 1024)


def solution(mesh):
    in_specs = (
        P(None, "col", "grp"),
        P(("grp", "col"), None, None),
        P(("grp", "col"), None, None),
        P("grp"),
        P("grp"),
        P(),
    )
    out_specs = P(None, "col", "grp")
    return jax.shard_map(on_device, mesh=mesh, in_specs=in_specs, out_specs=out_specs, check_vma=False)
```

```python
import functools

import jax
import jax.numpy as jnp
from jax import lax
from jax.experimental import pallas as pl
from jax.experimental.pallas import tpu as pltpu
from jax.sharding import PartitionSpec as P


STEPS = 2
NZ, NX, NY = 8, 4, 4
NC = NZ * NX * 2
MIB = 1024 * 1024
F32, BF16 = jnp.float32, jnp.bfloat16
ROWS, STRIP = 512, 64
PER, ALL, HALF = 208, 416, 512


def sds(*shape, dtype=BF16):
    return jax.ShapeDtypeStruct(shape, dtype)


def shift(axis, s):
    pairs = []
    for c in range(NC):
        z, x, k = c // (2 * NX), (c // 2) % NX, c % 2
        z, x = ((z + s) % NZ, x) if axis == "z" else (z, (x + s) % NX)
        pairs.append((c, (z * NX + x) * 2 + k))
    return pairs


def move(a, axis, s):
    if axis == "y":
        return lax.ppermute(a, "grp", [(i, (i + s) % NY) for i in range(NY)])
    return lax.ppermute(a, "col", shift(axis, s))


def swap_cores(a):
    return lax.ppermute(a, "col", [(c, c ^ 1) for c in range(NC)])


def turn(a, axis):
    if axis == "x":
        ahead, back = shift("x", 1), shift("x", -1)
        return lax.ppermute(a, "col", [(ahead, back)[c % 2][c] for c in range(NC)])
    pairs = [(g * NC + c, (g + 1 - 2 * (c % 2)) % NY * NC + c) for g in range(NY) for c in range(NC)]
    return lax.ppermute(a, ("grp", "col"), pairs)


def around(a, axis, n):
    out = [a]
    for _ in range(n - 1):
        out.append(turn(out[-1], axis))
    return out


def halves(p, m):
    h = p.shape[0] // 2

    def kernel(p, m, a, b):
        a[...] = p[:h]
        b[...] = m[p.shape[0] - h :]

    shape = sds(h, *p.shape[1:])
    return call(kernel, [p, m], (shape, shape), moved=4 * shape.size)


def ring(a, axis, n):
    out, p, m = [a], a, a
    for _ in range(n // 2 - 1):
        p, m = move(p, axis, 1), move(m, axis, -1)
        out += [p, m]
    p, m = halves(p, m)
    return out + [move(p, axis, 1), move(m, axis, -1)]


def spec(a):
    return pl.BlockSpec(memory_space=pltpu.SMEM if a.dtype == jnp.int32 else pltpu.VMEM)


def call(kernel, args, out_shape, flops=0, moved=0, aliases=None, limit=16):
    return pl.pallas_call(
        kernel,
        out_shape=out_shape,
        in_specs=[spec(a) for a in args],
        out_specs=jax.tree.map(spec, out_shape),
        input_output_aliases=aliases or {},
        compiler_params=pltpu.CompilerParams(vmem_limit_bytes=limit * MIB),
        cost_estimate=pl.CostEstimate(flops=flops, bytes_accessed=moved, transcendentals=0),
    )(*args)


def join(pieces):
    def kernel(*refs):
        at = 0
        for ref in refs[:-1]:
            n = ref.shape[0]
            refs[-1][at : at + n] = ref[...]
            at += n

    n = sum(p.shape[0] for p in pieces)
    shape = sds(n, *pieces[0].shape[1:])
    return call(kernel, pieces, shape, moved=2 * shape.size)


def halve_tiles(kv, c, s):
    def kernel(kv, c, s, keep, send):
        k = kv[0]
        for i, t in enumerate((c, s)):
            keep[i] = t[0, pl.ds(pl.multiple_of(k * 128, 128), 128), :]
            send[i] = t[0, pl.ds(pl.multiple_of((1 - k) * 128, 128), 128), :]

    return call(kernel, [kv, c, s], (sds(2, 128, 256), sds(2, 128, 256)), moved=MIB // 2)


def pair_tiles(keep, got):
    def kernel(keep, got, c, s):
        c[0], c[1], s[0], s[1] = keep[0], got[0], keep[1], got[1]

    return call(kernel, [keep, got], (sds(2, 128, 256), sds(2, 128, 256)), moved=MIB // 2)


def lanes(r, side):
    return pl.ds(pl.multiple_of(r * 256 + side * 128, 128), 128)


def split_columns(kv, o):
    def kernel(kv, o, keep, send):
        k = kv[0]
        for r in range(4):
            keep[:, r * 128 : (r + 1) * 128] = o[:, lanes(r, k)]
            send[:, r * 128 : (r + 1) * 128] = o[:, lanes(r, 1 - k)]

    return call(kernel, [kv, o], (sds(PER, HALF), sds(PER, HALF)), moved=MIB)


def own_rows(k):
    return pl.ds(pl.multiple_of(k * PER, PER), PER)


def stack_cores(kv, keep, got):
    def kernel(kv, keep, got, out, top, bottom):
        out[own_rows(kv[0]), :] = keep[...]
        out[own_rows(1 - kv[0]), :] = got[...]
        top[...] = out[:PER, :]
        bottom[...] = out[PER:, :]

    shapes = (sds(ALL, HALF), sds(PER, HALF), sds(PER, HALF))
    return call(kernel, [kv, keep, got], shapes, moved=MIB)


def merge_columns(kv, mine, got):
    def kernel(kv, mine, got, out):
        k = kv[0]
        for r in range(4):
            out[:, lanes(r, k)] = mine[:, r * 128 : (r + 1) * 128]
            out[:, lanes(r, 1 - k)] = got[:, r * 128 : (r + 1) * 128]

    return call(kernel, [kv, mine, got], sds(PER, 1024), moved=MIB)


def add_tiles(meta, pieces, acc, at):
    for ref in pieces:
        def add(t, _, ref=ref, at=at):
            r = meta[0, at + t]

            @pl.when(r >= 0)
            def _():
                row = pl.ds(pl.multiple_of(r * 128, 128), 128)
                for h in range(2):
                    lane = pl.ds(pl.multiple_of(meta[1 + h, at + t] * 128, 128), 128)
                    acc[row, lane] += ref[t, :, h * 128 : (h + 1) * 128].astype(F32)

            return 0

        lax.fori_loop(0, ref.shape[0], add, 0)
        at += ref.shape[0]


def strips(body):
    def one(i, _):
        body(pl.ds(pl.multiple_of(i * STRIP, STRIP), STRIP))
        return 0

    lax.fori_loop(0, ROWS // STRIP, one, 0)


def scatter(meta, pieces, late):
    def first(meta, *refs):
        acc = refs[-1]

        def clear(row):
            acc[row, :] = jnp.zeros((STRIP, acc.shape[1]), F32)

        strips(clear)
        add_tiles(meta, refs[:-1], acc, 0)

    at = sum(p.shape[0] for p in pieces)

    def second(meta, before, *refs):
        acc, out = refs[-2], refs[-1]
        add_tiles(meta, refs[:-2], acc, at)

        def rounded(row):
            out[row, :] = acc[row, :].astype(BF16)

        strips(rounded)

    full = sds(ROWS, 4096, dtype=F32)
    acc = call(first, [meta] + pieces, full, moved=8 * MIB)
    return call(second, [meta, acc] + late, (full, sds(ROWS, 4096)), moved=4 * MIB, aliases={1: 0})[1]


def nt(a, b):
    return lax.dot_general(a, b, (((1,), (1,)), ((), ())), preferred_element_type=F32)


def products(kv, own, other, first, mats, acc=None, cur=None, last=None):
    nm, blocks = len(mats), own.shape[0] // ALL

    def kernel(kv, own, other, *refs):
        ms, rest = refs[:nm], list(refs[nm:])
        before = rest.pop(0) if acc is not None else None
        prev = (rest.pop(0), rest.pop(0)) if cur is not None else None

        def sums(m, cols):
            total = None
            for i in range(blocks):
                for h, x in enumerate((own, other)):
                    q = ((first + i) * 2 + h) * HALF
                    d = nt(x[i * ALL : (i + 1) * ALL, :], m[cols, q : q + HALF])
                    total = d if total is None else total + d
            return total

        def body(j, _):
            cols = pl.ds(pl.multiple_of(j * 256, 256), 256)
            t = sums(ms[0], cols)
            if nm == 2:
                s = sums(ms[1], cols)
                n = PER // 2
                t = jnp.concatenate(
                    [t[:n] + s[n : 2 * n], t[n : 2 * n] - s[:n], t[2 * n : 3 * n] + s[3 * n :], t[3 * n :] - s[2 * n : 3 * n]],
                    axis=0,
                )
            if before is not None:
                t = t + before[:, cols]
            if prev is not None:
                t = 2.0 * t - jnp.concatenate([v[:, cols].astype(F32) for v in prev], axis=0)
            if last is None:
                rest[0][:, cols] = t
            else:
                t = t.astype(BF16)
                a, b = t[:PER], t[PER:]
                if last == "rows":
                    a, b = jnp.where(kv[0] == 0, a, b), jnp.where(kv[0] == 0, b, a)
                rest[0][:, cols] = a
                rest[1][:, cols] = b
            return 0

        lax.fori_loop(0, 2, body, 0)

    args = [kv, own, other] + list(mats) + ([] if acc is None else [acc]) + list(cur or ())
    shape = (sds(PER, HALF),) * 2 if last else sds(ALL, HALF, dtype=F32)
    flops = 4 * ALL * HALF * HALF * blocks * nm
    return call(kernel, args, shape, flops=flops, moved=2 * MIB * nm)


def exchange(v):
    t, b = v
    pt, mb = move(t, "y", 1), move(b, "y", -1)
    pb, mt = move(b, "y", 1), move(t, "y", -1)
    fp, fm = move(pt, "y", 1), move(mb, "y", -1)
    near = join([t, b, pt, pb, mt, mb])
    near_o = swap_cores(near)
    far = join([fp, fm])
    return near, near_o, far, swap_cores(far)


def first_exchange(kv, v):
    t = around(v, "y", NY)

    def kernel(kv, v, a, b, c, near, far):
        k = kv[0]
        near[:ALL] = v[...]
        near[pl.ds(pl.multiple_of(ALL + k * ALL, ALL), ALL), :] = a[...]
        near[pl.ds(pl.multiple_of(2 * ALL - k * ALL, ALL), ALL), :] = c[...]
        far[...] = b[...]

    near, far = call(kernel, [kv] + t, (sds(3 * ALL, HALF), sds(ALL, HALF)), moved=4 * MIB)
    return near, swap_cores(near), far, swap_cores(far)


def stage(kv, ex, mats, cur=None, last="all"):
    near, near_o, far, far_o = ex
    acc = products(kv, near, near_o, 0, mats)
    return products(kv, far, far_o, 3, mats, acc=acc, cur=cur, last=last)


def on_device(orbitals, cosine_tiles, sine_tiles, tile_row, tile_col, row_place):
    col = lax.axis_index("col")
    grp = lax.axis_index("grp")
    k = col % 2
    z, x = col // (2 * NX), (col // 2) % NX
    kv = k.astype(jnp.int32)[None]

    keep, send = halve_tiles(kv, cosine_tiles, sine_tiles)
    c2, s2 = pair_tiles(keep, swap_cores(send))
    cz = ring(c2, "z", NZ)
    ca = ring(join(cz[:5]), "x", NX)
    cb = ring(join(cz[5:]), "x", NX)
    s8 = join(around(s2, "x", NX))
    s_all = ring(s8, "z", NZ)
    keep_o, send_o = split_columns(kv, orbitals.reshape(PER, 1024))
    cur, top, bottom = stack_cores(kv, keep_o, swap_cores(send_o))
    ex = first_exchange(kv, cur)
    cur = (top, bottom)

    def meta_of(zs, xs):
        slot = ((z + zs) % NZ * NX + (x + xs) % NX) * 2 + (k ^ (jnp.arange(64, dtype=jnp.int32) % 2))
        hit = slot[:, None] == jnp.arange(64, dtype=jnp.int32)[None, :]
        row = jnp.sum(jnp.where(hit, tile_row[None, :], 0), axis=1)
        tcol = jnp.sum(jnp.where(hit, tile_col[None, :], 0), axis=1)
        blk = jnp.sum(
            jnp.where(tcol[:, None] == jnp.arange(16, dtype=jnp.int32)[None, :], row_place[None, :], 0), axis=1
        )
        d = (blk // 4 - grp) % 4
        grel = jnp.where(d == 0, 0, jnp.where(d == 3, 1, d + 1))
        base = grel * 8 + blk % 4
        return jnp.stack([row, base + 4 * k, base + 4 * (1 - k)]).astype(jnp.int32)

    i32 = functools.partial(jnp.array, dtype=jnp.int32)
    za, zb = [0, 0, -1, -1, 1, 1, -2, -2, 2, 2], [-3, -3, 3, 3, 4, 4]
    xf = [0, -1, 1]
    c_meta = meta_of(i32(za * 4 + zb * 4), i32([d for d in xf + [2] for _ in za] + [d for d in xf + [2] for _ in zb]))
    zr = [0, -1, 1, -2, 2, -3, 3, 4]
    xr = (2 * k - 1).astype(jnp.int32) * i32([0, 0, 1, 1, 2, 2, 3, 3] * 8)
    s_meta = meta_of(i32([d for d in zr for _ in range(8)]), xr)

    c_mat = scatter(c_meta, ca + cb[:3], cb[3:])
    spread = stage(kv, ex, [c_mat])
    s_mat = scatter(s_meta, s_all[:7], s_all[7:])
    for update in range(STEPS):
        if update:
            ex = exchange(cur)
            spread = stage(kv, ex, [c_mat])
        last = "rows" if update == STEPS - 1 else "all"
        ex = exchange(spread)
        cur = stage(kv, ex, [c_mat, s_mat], cur=cur, last=last)
    mine, away = cur
    return merge_columns(kv, mine, swap_cores(away)).reshape(2, 104, 1024)


def solution(mesh):
    in_specs = (
        P(None, "col", "grp"),
        P(("grp", "col"), None, None),
        P(("grp", "col"), None, None),
        P("grp"),
        P("grp"),
        P(),
    )
    out_specs = P(None, "col", "grp")
    return jax.shard_map(on_device, mesh=mesh, in_specs=in_specs, out_specs=out_specs, check_vma=False)
```

```python
import functools

import jax
import jax.numpy as jnp
from jax import lax
from jax.experimental import pallas as pl
from jax.experimental.pallas import tpu as pltpu
from jax.sharding import PartitionSpec as P


STEPS = 2
NZ, NX, NY = 8, 4, 4
NC = NZ * NX * 2
MIB = 1024 * 1024
F32, BF16 = jnp.float32, jnp.bfloat16
ROWS, STRIP = 512, 64
PER, ALL, HALF = 208, 416, 512


def sds(*shape, dtype=BF16):
    return jax.ShapeDtypeStruct(shape, dtype)


def shift(axis, s):
    pairs = []
    for c in range(NC):
        z, x, k = c // (2 * NX), (c // 2) % NX, c % 2
        z, x = ((z + s) % NZ, x) if axis == "z" else (z, (x + s) % NX)
        pairs.append((c, (z * NX + x) * 2 + k))
    return pairs


def move(a, axis, s):
    if axis == "y":
        return lax.ppermute(a, "grp", [(i, (i + s) % NY) for i in range(NY)])
    return lax.ppermute(a, "col", shift(axis, s))


def swap_cores(a):
    return lax.ppermute(a, "col", [(c, c ^ 1) for c in range(NC)])


def turn(a, axis):
    if axis == "x":
        ahead, back = shift("x", 1), shift("x", -1)
        return lax.ppermute(a, "col", [(ahead, back)[c % 2][c] for c in range(NC)])
    pairs = [(g * NC + c, (g + 1 - 2 * (c % 2)) % NY * NC + c) for g in range(NY) for c in range(NC)]
    return lax.ppermute(a, ("grp", "col"), pairs)


def around(a, axis, n):
    out = [a]
    for _ in range(n - 1):
        out.append(turn(out[-1], axis))
    return out


def halves(p, m):
    h = p.shape[0] // 2

    def kernel(p, m, a, b):
        a[...] = p[:h]
        b[...] = m[p.shape[0] - h :]

    shape = sds(h, *p.shape[1:])
    return call(kernel, [p, m], (shape, shape), moved=4 * shape.size)


def ring(a, axis, n):
    out, p, m = [a], a, a
    for _ in range(n // 2 - 1):
        p, m = move(p, axis, 1), move(m, axis, -1)
        out += [p, m]
    p, m = halves(p, m)
    return out + [move(p, axis, 1), move(m, axis, -1)]


def ring_x(a, b):
    got = []
    for v in (a, b):
        got.append((move(v, "x", 1), move(v, "x", -1)))
    (ap, am), (bp, bm) = got
    i, j = a.shape[0] // 2, b.shape[0] // 2

    def kernel(ap, am, bp, bm, p, m):
        p[:i], p[i:] = ap[:i], bp[:j]
        m[:i], m[i:] = am[i:], bm[j:]

    shape = sds(i + j, *a.shape[1:])
    p, m = call(kernel, [ap, am, bp, bm], (shape, shape), moved=4 * shape.size)
    far = [move(p, "x", 1), move(m, "x", -1)]
    return [a, ap, am, b, bp, bm], far


def spec(a):
    return pl.BlockSpec(memory_space=pltpu.SMEM if a.dtype == jnp.int32 else pltpu.VMEM)


def call(kernel, args, out_shape, flops=0, moved=0, aliases=None, limit=16):
    return pl.pallas_call(
        kernel,
        out_shape=out_shape,
        in_specs=[spec(a) for a in args],
        out_specs=jax.tree.map(spec, out_shape),
        input_output_aliases=aliases or {},
        compiler_params=pltpu.CompilerParams(vmem_limit_bytes=limit * MIB),
        cost_estimate=pl.CostEstimate(flops=flops, bytes_accessed=moved, transcendentals=0),
    )(*args)


def join(pieces):
    def kernel(*refs):
        at = 0
        for ref in refs[:-1]:
            n = ref.shape[0]
            refs[-1][at : at + n] = ref[...]
            at += n

    n = sum(p.shape[0] for p in pieces)
    shape = sds(n, *pieces[0].shape[1:])
    return call(kernel, pieces, shape, moved=2 * shape.size)


def halve_tiles(kv, c, s):
    def kernel(kv, c, s, keep, send):
        k = kv[0]
        for i, t in enumerate((c, s)):
            keep[i] = t[0, pl.ds(pl.multiple_of(k * 128, 128), 128), :]
            send[i] = t[0, pl.ds(pl.multiple_of((1 - k) * 128, 128), 128), :]

    return call(kernel, [kv, c, s], (sds(2, 128, 256), sds(2, 128, 256)), moved=MIB // 2)


def pair_tiles(keep, got):
    def kernel(keep, got, c, s):
        c[0], c[1], s[0], s[1] = keep[0], got[0], keep[1], got[1]

    return call(kernel, [keep, got], (sds(2, 128, 256), sds(2, 128, 256)), moved=MIB // 2)


def lanes(r, side):
    return pl.ds(pl.multiple_of(r * 256 + side * 128, 128), 128)


def split_columns(kv, o):
    def kernel(kv, o, keep, send):
        k = kv[0]
        for r in range(4):
            keep[:, r * 128 : (r + 1) * 128] = o[:, lanes(r, k)]
            send[:, r * 128 : (r + 1) * 128] = o[:, lanes(r, 1 - k)]

    return call(kernel, [kv, o], (sds(PER, HALF), sds(PER, HALF)), moved=MIB)


def own_rows(k):
    return pl.ds(pl.multiple_of(k * PER, PER), PER)


def stack_cores(kv, keep, got):
    def kernel(kv, keep, got, out, top, bottom):
        out[own_rows(kv[0]), :] = keep[...]
        out[own_rows(1 - kv[0]), :] = got[...]
        top[...] = out[:PER, :]
        bottom[...] = out[PER:, :]

    shapes = (sds(ALL, HALF), sds(PER, HALF), sds(PER, HALF))
    return call(kernel, [kv, keep, got], shapes, moved=MIB)


def merge_columns(kv, mine, got):
    def kernel(kv, mine, got, out):
        k = kv[0]
        for r in range(4):
            out[:, lanes(r, k)] = mine[:, r * 128 : (r + 1) * 128]
            out[:, lanes(r, 1 - k)] = got[:, r * 128 : (r + 1) * 128]

    return call(kernel, [kv, mine, got], sds(PER, 1024), moved=MIB)


def add_tiles(meta, pieces, acc, at):
    for ref in pieces:
        def add(t, _, ref=ref, at=at):
            r = meta[0, at + t]

            @pl.when(r >= 0)
            def _():
                row = pl.ds(pl.multiple_of(r * 128, 128), 128)
                for h in range(2):
                    lane = pl.ds(pl.multiple_of(meta[1 + h, at + t] * 128, 128), 128)
                    acc[row, lane] += ref[t, :, h * 128 : (h + 1) * 128].astype(F32)

            return 0

        lax.fori_loop(0, ref.shape[0], add, 0, unroll=2)
        at += ref.shape[0]


def strips(body):
    def one(i, _):
        body(pl.ds(pl.multiple_of(i * STRIP, STRIP), STRIP))
        return 0

    lax.fori_loop(0, ROWS // STRIP, one, 0)


def scatter(meta, pieces, late):
    def first(meta, *refs):
        acc = refs[-1]

        def clear(row):
            acc[row, :] = jnp.zeros((STRIP, acc.shape[1]), F32)

        strips(clear)
        add_tiles(meta, refs[:-1], acc, 0)

    at = sum(p.shape[0] for p in pieces)

    def second(meta, before, *refs):
        acc, out = refs[-2], refs[-1]
        add_tiles(meta, refs[:-2], acc, at)

        def rounded(row):
            out[row, :] = acc[row, :].astype(BF16)

        strips(rounded)

    full = sds(ROWS, 4096, dtype=F32)
    acc = call(first, [meta] + pieces, full, moved=8 * MIB)
    return call(second, [meta, acc] + late, (full, sds(ROWS, 4096)), moved=4 * MIB, aliases={1: 0})[1]


def nt(a, b):
    return lax.dot_general(a, b, (((1,), (1,)), ((), ())), preferred_element_type=F32)


def products(kv, own, other, first, mats, acc=None, cur=None, last=None):
    nm, blocks = len(mats), own.shape[0] // ALL

    def kernel(kv, own, other, *refs):
        ms, rest = refs[:nm], list(refs[nm:])
        before = rest.pop(0) if acc is not None else None
        prev = (rest.pop(0), rest.pop(0)) if cur is not None else None

        def sums(m, cols):
            total = None
            for i in range(blocks):
                for h, x in enumerate((own, other)):
                    q = ((first + i) * 2 + h) * HALF
                    d = nt(x[i * ALL : (i + 1) * ALL, :], m[cols, q : q + HALF])
                    total = d if total is None else total + d
            return total

        def body(j, _):
            cols = pl.ds(pl.multiple_of(j * 256, 256), 256)
            t = sums(ms[0], cols)
            if nm == 2:
                s = sums(ms[1], cols)
                n = PER // 2
                t = jnp.concatenate(
                    [t[:n] + s[n : 2 * n], t[n : 2 * n] - s[:n], t[2 * n : 3 * n] + s[3 * n :], t[3 * n :] - s[2 * n : 3 * n]],
                    axis=0,
                )
            if before is not None:
                t = t + before[:, cols]
            if prev is not None:
                t = 2.0 * t - jnp.concatenate([v[:, cols].astype(F32) for v in prev], axis=0)
            if last is None:
                rest[0][:, cols] = t
            else:
                t = t.astype(BF16)
                a, b = t[:PER], t[PER:]
                if last == "rows":
                    a, b = jnp.where(kv[0] == 0, a, b), jnp.where(kv[0] == 0, b, a)
                rest[0][:, cols] = a
                rest[1][:, cols] = b
            return 0

        lax.fori_loop(0, 2, body, 0)

    args = [kv, own, other] + list(mats) + ([] if acc is None else [acc]) + list(cur or ())
    shape = (sds(PER, HALF),) * 2 if last else sds(ALL, HALF, dtype=F32)
    flops = 4 * ALL * HALF * HALF * blocks * nm
    return call(kernel, args, shape, flops=flops, moved=2 * MIB * nm)


def exchange(v):
    t, b = v
    pt, mb = move(t, "y", 1), move(b, "y", -1)
    pb, mt = move(b, "y", 1), move(t, "y", -1)
    fp, fm = move(pt, "y", 1), move(mb, "y", -1)
    near = join([t, b, pt, pb, mt, mb])
    near_o = swap_cores(near)
    far = join([fp, fm])
    return near, near_o, far, swap_cores(far)


def first_exchange(kv, v):
    t = around(v, "y", NY)

    def kernel(kv, v, a, c, near):
        k = kv[0]
        near[:ALL] = v[...]
        near[pl.ds(pl.multiple_of(ALL + k * ALL, ALL), ALL), :] = a[...]
        near[pl.ds(pl.multiple_of(2 * ALL - k * ALL, ALL), ALL), :] = c[...]

    far = t[2]
    near = call(kernel, [kv, t[0], t[1], t[3]], sds(3 * ALL, HALF), moved=3 * MIB)
    return near, swap_cores(near), far, swap_cores(far)


def stage(kv, ex, mats, cur=None, last="all"):
    near, near_o, far, far_o = ex
    acc = products(kv, near, near_o, 0, mats)
    return products(kv, far, far_o, 3, mats, acc=acc, cur=cur, last=last)


def on_device(orbitals, cosine_tiles, sine_tiles, tile_row, tile_col, row_place):
    col = lax.axis_index("col")
    grp = lax.axis_index("grp")
    k = col % 2
    z, x = col // (2 * NX), (col // 2) % NX
    kv = k.astype(jnp.int32)[None]

    keep, send = halve_tiles(kv, cosine_tiles, sine_tiles)
    c2, s2 = pair_tiles(keep, swap_cores(send))
    cz = ring(c2, "z", NZ)
    c_near, c_far = ring_x(join(cz[:5]), join(cz[5:]))
    s8 = join(around(s2, "x", NX))
    s_all = ring(s8, "z", NZ)
    keep_o, send_o = split_columns(kv, orbitals.reshape(PER, 1024))
    cur, top, bottom = stack_cores(kv, keep_o, swap_cores(send_o))
    ex = first_exchange(kv, cur)
    cur = (top, bottom)

    def meta_of(zs, xs, which):
        slot = ((z + zs) % NZ * NX + (x + xs) % NX) * 2 + (k ^ which)
        hit = slot[:, None] == jnp.arange(64, dtype=jnp.int32)[None, :]
        row = jnp.sum(jnp.where(hit, tile_row[None, :], 0), axis=1)
        tcol = jnp.sum(jnp.where(hit, tile_col[None, :], 0), axis=1)
        blk = jnp.sum(
            jnp.where(tcol[:, None] == jnp.arange(16, dtype=jnp.int32)[None, :], row_place[None, :], 0), axis=1
        )
        d = (blk // 4 - grp) % 4
        grel = jnp.where(d == 0, 0, jnp.where(d == 3, 1, d + 1))
        base = grel * 8 + blk % 4
        return jnp.stack([row, base + 4 * k, base + 4 * (1 - k)]).astype(jnp.int32)

    i32 = functools.partial(jnp.array, dtype=jnp.int32)
    za, zb = [0, 0, -1, -1, 1, 1, -2, -2, 2, 2], [-3, -3, 3, 3, 4, 4]
    xf = [0, -1, 1]
    far = za[:5] + zb[:3] + za[5:] + zb[3:]
    xs = [d for d in xf for _ in za] + [d for d in xf for _ in zb] + [2] * 16
    wa, wb = [0, 1] * 5, [0, 1] * 3
    which = wa * 3 + wb * 3 + wa[:5] + wb[:3] + wa[5:] + wb[3:]
    c_meta = meta_of(i32(za * 3 + zb * 3 + far), i32(xs), i32(which))
    zr = [0, -1, 1, -2, 2, -3, 3, 4]
    xr = (2 * k - 1).astype(jnp.int32) * i32([0, 0, 1, 1, 2, 2, 3, 3] * 8)
    s_meta = meta_of(i32([d for d in zr for _ in range(8)]), xr, i32([0, 1] * 32))

    c_mat = scatter(c_meta, c_near, c_far)
    spread = stage(kv, ex, [c_mat])
    s_mat = scatter(s_meta, s_all[:7], s_all[7:])
    for update in range(STEPS):
        if update:
            ex = exchange(cur)
            spread = stage(kv, ex, [c_mat])
        last = "rows" if update == STEPS - 1 else "all"
        ex = exchange(spread)
        cur = stage(kv, ex, [c_mat, s_mat], cur=cur, last=last)
    mine, away = cur
    return merge_columns(kv, mine, swap_cores(away)).reshape(2, 104, 1024)


def solution(mesh):
    in_specs = (
        P(None, "col", "grp"),
        P(("grp", "col"), None, None),
        P(("grp", "col"), None, None),
        P("grp"),
        P("grp"),
        P(),
    )
    out_specs = P(None, "col", "grp")
    return jax.shard_map(on_device, mesh=mesh, in_specs=in_specs, out_specs=out_specs, check_vma=False)
```
